32 devices in a mesh: dp: 2 (over x), tensor: 8 (over z, y), pipe: 2 (over core).
Axes of the slice: x: 2, y: 2, z: 4, core: 2. Of those that a mesh axis runs over, the one named last changes fastest.
Arguments:
- hidden: bfloat16 [2, 1024, 7168], P('pipe', ('dp', 'tensor')), may hold values from -200 to 200
- head_table: bfloat16 [81920, 7168], P(('dp', 'tensor')), may hold values from -1 to 1
- targets: int32 [2, 1024], P('pipe', ('dp', 'tensor')), may hold values from 0 to 81919
Outputs:
- token_loss: float32 [2, 1024], P('pipe', ('dp', 'tensor'))
- mean_loss: float32 [], replicated
The draws below stay inside these ranges and needn't reach their ends.
All inputs are finite; a program needn't handle non-finite values.
Results may differ from the reference program's by a relative error of at most 0.0003.
Values may be sent and summed in bfloat16 or wider, within the bound.
No kernel may reach another device: no remote copies, remote signals or barrier semaphores. Data moves between devices by JAX's collectives and lax.ppermute only.
A program may use at most 192 MiB of HBM per device.

```python
import math
import jax
import jax.numpy as jnp
from jax import lax

D = 7168
V = 81920
GROUP = 1024
MICRO = 2


def table_row(key, row_index):
    base_key = jax.random.fold_in(key, 7001)
    values = jax.random.normal(jax.random.fold_in(base_key, row_index), (D,), jnp.float32) / math.sqrt(D)
    limit = 6.0 / math.sqrt(D)
    return jnp.clip(values, -limit, limit).astype(jnp.bfloat16).astype(jnp.float32)


def draw_head_table(key, part):
    return jax.vmap(lambda row_index: table_row(key, row_index))(jnp.arange(V)).astype(jnp.bfloat16)


def draw_hidden(key, part):
    own_key = jax.random.fold_in(key, 7002)
    keys = jax.random.split(own_key, 3)
    group_count = MICRO
    group_rise = 3.0 ** (jnp.arange(group_count, dtype=jnp.float32) / max(group_count - 1, 1))
    base_values = jax.random.normal(keys[0], (group_count, GROUP, D), jnp.float32)
    row_scale = jnp.exp(jax.random.uniform(keys[2], (group_count, GROUP, 1), jnp.float32, 0.0, math.log(3.0)))
    states = base_values * 1.5 * row_scale * group_rise[:, None, None]
    return jnp.clip(states, -200.0, 200.0).astype(jnp.bfloat16)


def touch_ends(values, key, least, top_value):
    extent = values.shape
    place = [jax.random.randint(jax.random.fold_in(key, axis), (), 0, extent[axis]) for axis in range(len(extent))]
    values = values.at[tuple(place)].set(least)
    longest = extent.index(max(extent))
    place[longest] = (place[longest] + 1) % extent[longest]
    return values.at[tuple(place)].set(top_value)


def setup_inputs(seed: int = 0) -> dict:
    streams_of = jax.random.split(jax.random.key(seed), 4)
    return {
        "hidden": draw_hidden(jax.random.fold_in(streams_of[3], 71), 0),
        "head_table": draw_head_table(jax.random.fold_in(streams_of[3], 71), 0),
        "targets": touch_ends(jax.random.randint(streams_of[2], (MICRO, GROUP), 0, V), jax.random.fold_in(streams_of[2], 1), 0, V - 1).astype(jnp.int32),
    }


def block_losses(token_block, label_block, head_table):
    logits = lax.dot_general(token_block, head_table, (((1,), (1,)), ((), ())), preferred_element_type=jnp.float32)
    maxima = jnp.max(logits, axis=1)
    sums = jnp.sum(jnp.exp(logits - maxima[:, None]), axis=1)
    columns = lax.broadcasted_iota(jnp.int32, logits.shape, 1)
    picked = jnp.sum(jnp.where(columns == label_block.astype(jnp.int32)[:, None], logits, jnp.zeros_like(logits)), axis=1)
    return maxima + jnp.log(sums) - picked


def reference(hidden, head_table, targets):
    pipe_count, group_size, model_width = hidden.shape
    all_tokens = pipe_count * group_size
    block_rows = math.gcd(all_tokens, 128)
    flat_rows = hidden.reshape(all_tokens // block_rows, block_rows, model_width)
    flat_labels = targets.reshape(all_tokens // block_rows, block_rows)
    losses = lax.map(lambda block_pair: block_losses(block_pair[0], block_pair[1], head_table), (flat_rows, flat_labels))
    token_loss = losses.reshape(pipe_count, group_size)
    mean_loss = jnp.sum(token_loss) / all_tokens
    return token_loss, mean_loss
```

```python
import functools

import jax
import jax.numpy as jnp
from jax import lax
from jax.experimental import pallas as pl
from jax.experimental.pallas import tpu as pltpu
from jax.sharding import PartitionSpec as P

AXES = ("dp", "tensor")
SUB = 8
LANES = 128
BASE = 256
LOWEST = -3.0e38
WEIGHTS = (4, 8, 8, 8)
MAX_TILE = 512
VMEM_LIMIT = 26 << 20


def head_kernel(cfg, *refs):
    refs = list(refs)
    take = lambda count: [refs.pop(0) for _ in range(count)]
    blocks = take(len(cfg["places"]))
    (table_ref,) = take(1)
    (sums_in,) = take(1) if cfg["has_sums"] else (None,)
    (labels_in,) = take(1) if cfg["last"] else (None,)
    (sums_out,) = (None,) if cfg["last"] else take(1)
    (labels_out,) = take(1) if cfg["first"] else (None,)
    if cfg["last"]:
        stats_out, max_ref, sum_ref, hit_ref = refs
    step = pl.program_id(0)
    tile, cols = table_ref.shape
    span = pl.ds(pl.multiple_of(step * tile, tile), tile)

    if cfg["last"]:

        @pl.when(step == 0)
        def _():
            max_ref[...] = jnp.full_like(max_ref, LOWEST)
            sum_ref[...] = jnp.zeros_like(sum_ref)
            hit_ref[...] = jnp.zeros_like(hit_ref)

    if cfg["first"]:

        @pl.when(step == 0)
        def _():
            for block, (source, own) in zip(blocks, cfg["places"]):
                digits = jnp.transpose(block[:, cols:].astype(jnp.float32))
                whole = (digits[0:1] * BASE + digits[1:2]) * BASE + digits[2:3]
                here = pl.ds(own, block.shape[0])
                labels_out[:, here] = jnp.broadcast_to(whole, (SUB, block.shape[0])).astype(jnp.int32)

    for block, (source, own) in zip(blocks, cfg["places"]):
        rows = block.shape[0]
        part = lax.dot_general(
            table_ref[...], block[:, :cols], (((1,), (1,)), ((), ())), preferred_element_type=jnp.float32
        )
        if cfg["adds"]:
            part = part + sums_in[span, pl.ds(source, rows)]
        if not cfg["last"]:
            sums_out[span, pl.ds(source, rows)] = part
            continue
        here = pl.ds(own, rows)
        groups = part.reshape(tile // SUB, SUB, rows)
        old = max_ref[:, here]
        new = jnp.maximum(old, jnp.max(groups, axis=0))
        near = labels_in[:1, pl.ds(source, rows)] - (cfg["offset_of"]() + step * tile)
        ids = lax.broadcasted_iota(jnp.int32, (tile, rows), 0)
        hits = jnp.where(ids == near, part, 0.0).reshape(tile // SUB, SUB, rows)
        sum_ref[:, here] = sum_ref[:, here] * jnp.exp(old - new) + jnp.sum(jnp.exp(groups - new[None]), axis=0)
        hit_ref[:, here] = hit_ref[:, here] + jnp.sum(hits, axis=0)
        max_ref[:, here] = new

    if cfg["last"]:

        @pl.when(step == pl.num_programs(0) - 1)
        def _():
            kept = max_ref[...]
            top = jnp.max(kept, axis=0, keepdims=True)
            total = jnp.sum(sum_ref[...] * jnp.exp(kept - top), axis=0, keepdims=True)
            hit = jnp.sum(hit_ref[...], axis=0, keepdims=True)
            row = lax.broadcasted_iota(jnp.int32, kept.shape, 0)
            stats_out[...] = jnp.where(row == 0, top, jnp.where(row == 1, total, hit))


def head_pass(blocks, sources, table, col, cols, tokens, sums=None, adds=False, labels=None, first=False, name=None):
    vocab = table.shape[0]
    last = labels is not None
    tile = max(t for t in range(16, MAX_TILE + 1, 16) if vocab % t == 0)
    rows = [b.shape[0] for b in blocks]
    owns = [sum(rows[:k]) for k in range(len(rows))]
    count = sum(rows)
    cfg = dict(
        places=list(zip(sources, sources if first else owns)),
        has_sums=sums is not None,
        adds=adds,
        last=last,
        first=first,
        offset_of=lambda: (lax.axis_index("dp") * lax.axis_size("tensor") + lax.axis_index("tensor")) * vocab,
    )
    near = pl.BlockSpec(memory_space=pltpu.VMEM)
    args = [*blocks, table]
    in_specs = [near] * len(blocks) + [pl.BlockSpec((pl.Element(tile), pl.Element(cols)), lambda i: (i * tile, col))]
    aliases = {}
    if sums is not None:
        if not last:
            aliases[len(args)] = 0
        args.append(sums)
        in_specs.append(near)
    scratch = []
    if last:
        args.append(labels)
        in_specs.append(near)
        out_shape = [jax.ShapeDtypeStruct((SUB, count), jnp.float32)]
        out_specs = [pl.BlockSpec((SUB, count), lambda i: (0, 0))]
        scratch = [pltpu.VMEM((SUB, count), jnp.float32)] * 3
    else:
        out_shape = [pltpu.VMEM((vocab, tokens), jnp.float32)]
        out_specs = [near]
        if first:
            out_shape.append(jax.ShapeDtypeStruct((SUB, tokens), jnp.int32))
            out_specs.append(near)
    return pl.pallas_call(
        functools.partial(head_kernel, cfg),
        out_shape=out_shape,
        grid=(vocab // tile,),
        in_specs=in_specs,
        out_specs=out_specs,
        scratch_shapes=scratch,
        input_output_aliases=aliases,
        compiler_params=pltpu.CompilerParams(dimension_semantics=("arbitrary",), vmem_limit_bytes=VMEM_LIMIT),
        cost_estimate=pl.CostEstimate(
            flops=2 * count * vocab * cols, bytes_accessed=2 * vocab * cols, transcendentals=0
        ),
        name=name,
    )(*args)


def swap(values, mask, devices):
    return lax.ppermute(values, AXES, [(i, i ^ mask) for i in range(devices)])


def merge(mine, other, upper):
    low = jnp.where(upper, other, mine)
    high = jnp.where(upper, mine, other)
    top = jnp.maximum(low[0], high[0])
    total = low[1] * jnp.exp(low[0] - top) + high[1] * jnp.exp(high[0] - top)
    return jnp.stack([top, total, low[2] + high[2]])


def body(mesh_shape, hidden, head_table, targets):
    devices = mesh_shape["dp"] * mesh_shape["tensor"]
    bits = devices.bit_length() - 1
    assert devices == 1 << bits and bits >= 2
    x_mask, y_mask = devices >> 1, 1
    z_masks = [1 << k for k in range(bits - 2, 0, -1)]
    own = hidden[0]
    own_count, width = own.shape
    tokens = own_count * devices
    quarter = tokens // 4
    half = quarter // 2
    position = lax.axis_index(AXES)

    ids = targets[0][:, None]
    digits = jnp.concatenate([ids // (BASE * BASE), ids // BASE % BASE, ids % BASE], axis=1).astype(own.dtype)
    digits = jnp.pad(digits, ((0, 0), (0, LANES - digits.shape[1])))

    units = width // LANES
    edges = [sum(WEIGHTS[:k]) * units // sum(WEIGHTS) * LANES for k in range(len(WEIGHTS) + 1)]
    sums = labels = None
    stats = []
    for k, (begin, end) in enumerate(zip(edges, edges[1:])):
        first, last = k == 0, k == len(WEIGHTS) - 1
        with jax.named_scope(f"gather_{k}"):
            column = own[:, begin:end]
            if first:
                column = jnp.concatenate([column, digits], axis=1)
            for mask in z_masks:
                column = jnp.concatenate([column, swap(column, mask, devices)], axis=0)
            from_x = swap(column, x_mask, devices)
            from_y = swap(column, y_mask, devices)
            far = [swap(from_x[:half], y_mask, devices), swap(from_y[half:], x_mask, devices)]
        call = functools.partial(head_pass, table=head_table, col=begin, cols=end - begin, tokens=tokens)
        if not last:
            out = call(
                [column, from_x, from_y, *far],
                [0, quarter, 2 * quarter, 3 * quarter, 3 * quarter + half],
                sums=sums,
                adds=not first,
                first=first,
                name=f"head_{k}",
            )
            sums = out[0]
            labels = out[1] if first else labels
        else:
            near = call(
                [column, from_x, from_y], [0, quarter, 2 * quarter], sums=sums, adds=True, labels=labels, name="head_near"
            )
            rest = call(far, [3 * quarter, 3 * quarter + half], sums=sums, adds=True, labels=labels, name="head_far")
            stats = [near[0], rest[0]]

    cells = 2 ** (bits - 2)
    state = jnp.concatenate([s[:3] for s in stats], axis=1)
    state = state.reshape((3, 2, 2) + (2,) * (bits - 2) + (own_count,))
    dims = [(x_mask, 2), (y_mask, 1)] + [(mask, len(z_masks) + 2 - j) for j, mask in enumerate(z_masks)]
    for mask, dim in dims:
        got = swap(state, mask, devices)
        state = merge(state, jnp.flip(got, axis=dim), (position & mask) != 0)
    losses = state[0] + jnp.log(state[1]) - state[2]
    own_losses = losses[(0,) * bits]
    block_sums = jnp.sum(losses, axis=-1)
    for _ in range(bits):
        block_sums = block_sums[0] + block_sums[1]
    loss_sum = lax.psum(block_sums, "pipe")
    mean_loss = loss_sum / (tokens * lax.axis_size("pipe"))
    return own_losses[None, :], mean_loss


def solution(mesh):
    in_specs = (P("pipe", AXES, None), P(AXES, None), P("pipe", AXES))
    out_specs = (P("pipe", AXES), P())
    run = functools.partial(body, dict(mesh.shape))
    return jax.shard_map(run, mesh=mesh, in_specs=in_specs, out_specs=out_specs, check_vma=False)
```

```python
import functools

import jax
import jax.numpy as jnp
from jax import lax
from jax.experimental import pallas as pl
from jax.experimental.pallas import tpu as pltpu
from jax.sharding import PartitionSpec as P


AXES = ("dp", "tensor")
SUB = 8
LANES = 128
BASE = 256
LOWEST = -3.0e38
WEIGHTS = (4, 6, 9, 9)
LABEL_CHUNK = 1
MAX_TILE = {"near": 512, "far": 1024}
VMEM_LIMIT = 16 << 20


def head_kernel(cfg, *refs):
    refs = list(refs)
    take = lambda count: [refs.pop(0) for _ in range(count)]
    blocks = take(len(cfg["places"]))
    (table_ref,) = take(1)
    (sums_in,) = take(1) if cfg["has_sums"] else (None,)
    (labels_in,) = take(1) if cfg["last"] else (None,)
    (sums_out,) = (None,) if cfg["last"] else take(1)
    (labels_out,) = take(1) if cfg["labels"] else (None,)
    (joined,) = take(1) if cfg["join"] and not cfg["last"] else (None,)
    if cfg["last"]:
        stats_out, max_ref, sum_ref, hit_ref = take(4)
        (joined,) = take(1) if cfg["join"] else (None,)
    step = pl.program_id(0)
    tile, cols = table_ref.shape
    span = pl.ds(pl.multiple_of(step * tile, tile), tile)

    if cfg["last"]:

        @pl.when(step == 0)
        def _():
            max_ref[...] = jnp.full_like(max_ref, LOWEST)
            sum_ref[...] = jnp.zeros_like(sum_ref)
            hit_ref[...] = jnp.zeros_like(hit_ref)

    if cfg["labels"]:

        @pl.when(step == 0)
        def _():
            for block, (source, own) in zip(blocks, cfg["places"]):
                digits = jnp.transpose(block[:, cols:].astype(jnp.float32))
                whole = (digits[0:1] * BASE + digits[1:2]) * BASE + digits[2:3]
                here = pl.ds(own, block.shape[0])
                labels_out[:, here] = jnp.broadcast_to(whole, (SUB, block.shape[0])).astype(jnp.int32)

    places = cfg["places"]
    if cfg["join"]:

        @pl.when(step == 0)
        def _():
            for block, (source, own) in zip(blocks, places):
                joined[pl.ds(own - places[0][1], block.shape[0]), :] = block[:, :cols]

        blocks, places = [joined], places[:1]

    for block, (source, own) in zip(blocks, places):
        rows = block.shape[0]
        part = lax.dot_general(
            table_ref[...], block[:, :cols], (((1,), (1,)), ((), ())), preferred_element_type=jnp.float32
        )
        if cfg["adds"]:
            part = part + sums_in[span, pl.ds(source, rows)]
        if not cfg["last"]:
            sums_out[span, pl.ds(source, rows)] = part
            continue
        here = pl.ds(own, rows)
        groups = part.reshape(tile // SUB, SUB, rows)
        old = max_ref[:, here]
        new = jnp.maximum(old, jnp.max(groups, axis=0))
        near = labels_in[:1, here] - (cfg["offset_of"]() + step * tile)
        ids = lax.broadcasted_iota(jnp.int32, (tile, rows), 0)
        hits = jnp.where(ids == near, part, 0.0).reshape(tile // SUB, SUB, rows)
        sum_ref[:, here] = sum_ref[:, here] * jnp.exp(old - new) + jnp.sum(jnp.exp(groups - new[None]), axis=0)
        hit_ref[:, here] = hit_ref[:, here] + jnp.sum(hits, axis=0)
        max_ref[:, here] = new

    if cfg["last"]:

        @pl.when(step == pl.num_programs(0) - 1)
        def _():
            kept = max_ref[...]
            top = jnp.max(kept, axis=0, keepdims=True)
            total = jnp.sum(sum_ref[...] * jnp.exp(kept - top), axis=0, keepdims=True)
            hit = jnp.sum(hit_ref[...], axis=0, keepdims=True)
            row = lax.broadcasted_iota(jnp.int32, kept.shape, 0)
            stats_out[...] = jnp.where(row == 0, top, jnp.where(row == 1, total, hit))


def head_pass(blocks, sources, table, col, cols, tokens, sums=None, adds=False, labels=None, emits=False, join=False, limit=512):
    vocab = table.shape[0]
    last = labels is not None
    tile = max(t for t in range(16, limit + 1, 16) if vocab % t == 0)
    rows = [b.shape[0] for b in blocks]
    owns = [sum(rows[:k]) for k in range(len(rows))]
    count = sum(rows)
    cfg = dict(
        places=list(zip(sources, owns)),
        has_sums=sums is not None,
        adds=adds,
        last=last,
        labels=emits,
        join=join,
        offset_of=lambda: (lax.axis_index("dp") * lax.axis_size("tensor") + lax.axis_index("tensor")) * vocab,
    )
    near = pl.BlockSpec(memory_space=pltpu.VMEM)
    args = [*blocks, table]
    in_specs = [near] * len(blocks) + [pl.BlockSpec((pl.Element(tile), pl.Element(cols)), lambda i: (i * tile, col))]
    aliases = {}
    if sums is not None:
        if not last:
            aliases[len(args)] = 0
        args.append(sums)
        in_specs.append(near)
    scratch = []
    if last:
        args.append(labels)
        in_specs.append(near)
        out_shape = [jax.ShapeDtypeStruct((SUB, count), jnp.float32)]
        out_specs = [pl.BlockSpec((SUB, count), lambda i: (0, 0))]
        scratch = [pltpu.VMEM((SUB, count), jnp.float32)] * 3
    else:
        out_shape = [pltpu.VMEM((vocab, tokens), jnp.float32)]
        out_specs = [near]
        if emits:
            out_shape.append(jax.ShapeDtypeStruct((SUB, count), jnp.int32))
            out_specs.append(near)
    if join:
        scratch.append(pltpu.VMEM((count, cols), table.dtype))
    return pl.pallas_call(
        functools.partial(head_kernel, cfg),
        out_shape=out_shape,
        grid=(vocab // tile,),
        in_specs=in_specs,
        out_specs=out_specs,
        scratch_shapes=scratch,
        input_output_aliases=aliases,
        compiler_params=pltpu.CompilerParams(dimension_semantics=("arbitrary",), vmem_limit_bytes=VMEM_LIMIT),
        cost_estimate=pl.CostEstimate(
            flops=2 * count * vocab * cols, bytes_accessed=2 * vocab * cols, transcendentals=0
        ),
    )(*args)


def swap(values, mask, devices):
    return lax.ppermute(values, AXES, [(i, i ^ mask) for i in range(devices)])


def merge(parts):
    top = functools.reduce(jnp.maximum, [p[0] for p in parts])
    totals = [p[1] * jnp.exp(p[0] - top) for p in parts]
    hits = [p[2] for p in parts]
    while len(totals) > 1:
        totals = [a + b for a, b in zip(totals[::2], totals[1::2])]
        hits = [a + b for a, b in zip(hits[::2], hits[1::2])]
    return jnp.stack([top, totals[0], hits[0]])


def body(mesh_shape, hidden, head_table, targets):
    devices = mesh_shape["dp"] * mesh_shape["tensor"]
    bits = devices.bit_length() - 1
    assert devices == 1 << bits and bits >= 2
    x_mask, y_mask = devices >> 1, 1
    z_masks = [1 << k for k in range(bits - 2, 0, -1)]
    own = hidden[0]
    own_count, width = own.shape
    tokens = own_count * devices
    quarter = tokens // 4
    half = quarter // 2

    ids = targets[0][:, None]
    digits = jnp.concatenate([ids // (BASE * BASE), ids // BASE % BASE, ids % BASE], axis=1).astype(own.dtype)
    digits = jnp.pad(digits, ((0, 0), (0, LANES - digits.shape[1])))

    units = width // LANES
    edges = [sum(WEIGHTS[:k]) * units // sum(WEIGHTS) * LANES for k in range(len(WEIGHTS) + 1)]
    sums, labels, stats = None, {}, []
    for k, (begin, end) in enumerate(zip(edges, edges[1:])):
        first, last = k == 0, k == len(WEIGHTS) - 1
        column = own[:, begin:end]
        if k == LABEL_CHUNK:
            column = jnp.concatenate([column, digits], axis=1)
        for mask in z_masks:
            column = jnp.concatenate([column, swap(column, mask, devices)], axis=0)
        from_x = swap(column, x_mask, devices)
        from_y = swap(column, y_mask, devices)
        far = [swap(from_x[:half], y_mask, devices), swap(from_y[half:], x_mask, devices)]
        groups = {
            "near": ([column, from_x, from_y], [0, quarter, 2 * quarter]),
            "far": (far, [3 * quarter, 3 * quarter + half]),
        }
        for group, (blocks, sources) in groups.items():
            out = head_pass(
                blocks,
                sources,
                head_table,
                begin,
                end - begin,
                tokens,
                sums=sums,
                adds=not first,
                labels=labels[group] if last else None,
                emits=k == LABEL_CHUNK,
                join=group == "far",
                limit=MAX_TILE[group],
            )
            if last:
                stats.append(out[0])
            else:
                sums = out[0]
            if k == LABEL_CHUNK:
                labels[group] = out[1]

    state = jnp.concatenate([s[:3] for s in stats], axis=1)
    state = state.reshape((3, 2, 2) + (2,) * (bits - 2) + (own_count,))
    dims = [(x_mask, 2), (y_mask, 1)] + [(mask, len(z_masks) + 2 - j) for j, mask in enumerate(z_masks)]
    for begin in range(0, len(dims), 2):
        pair = dims[begin : begin + 2]
        parts = [state]
        for take in range(1, 1 << len(pair)):
            used = [pair[j] for j in range(len(pair)) if take >> j & 1]
            mask = sum(m for m, _ in used)
            got = swap(state, mask, devices)
            parts.append(jnp.flip(got, axis=tuple(d for _, d in used)))
        state = merge(parts)
    losses = state[0] + jnp.log(state[1]) - state[2]
    own_losses = losses[(0,) * bits]
    block_sums = jnp.sum(losses, axis=-1)
    for _ in range(bits):
        block_sums = block_sums[0] + block_sums[1]
    loss_sum = lax.psum(block_sums, "pipe")
    mean_loss = loss_sum / (tokens * lax.axis_size("pipe"))
    return own_losses[None, :], mean_loss


def solution(mesh):
    in_specs = (P("pipe", AXES, None), P(AXES, None), P("pipe", AXES))
    out_specs = (P("pipe", AXES), P())

    def run(*args):
        return body(dict(mesh.shape), *args)

    return jax.shard_map(run, mesh=mesh, in_specs=in_specs, out_specs=out_specs, check_vma=False)
```

```python
import functools

import jax
import jax.numpy as jnp
from jax import lax
from jax.experimental import pallas as pl
from jax.experimental.pallas import tpu as pltpu
from jax.sharding import PartitionSpec as P


AXES = ("dp", "tensor")
SUB = 8
LANES = 128
BASE = 256
LOWEST = -3.0e38
WEIGHTS = (4, 6, 9, 9)
LABEL_CHUNK = 1
MAX_TILE = 512
DEPTH = 4
GROUPS = (("own", "rest"), ("all",), ("near", "far"), ("near", "far"))
VMEM_LIMIT = 18 << 20


def head_kernel(cfg, *refs):
    refs = list(refs)
    take = lambda count: [refs.pop(0) for _ in range(count)]
    blocks = take(len(cfg["places"]))
    (table_ref,) = take(1)
    (sums_in,) = take(1) if cfg["has_sums"] else (None,)
    (labels_in,) = take(1) if cfg["last"] else (None,)
    (out_ref,) = take(1)
    (labels_out,) = take(1) if cfg["labels"] else (None,)
    ring, arrived = take(2)
    (joined,) = take(1) if cfg["join"] else (None,)
    max_ref, sum_ref, hit_ref = take(3) if cfg["last"] else (None, None, None)
    _, tile, cols = ring.shape
    steps = table_ref.shape[0] // tile

    def fetch(step, slot):
        rows = pl.ds(pl.multiple_of(step * tile, tile), tile)
        return pltpu.make_async_copy(table_ref.at[rows, pl.ds(cfg["col"], cols)], ring.at[slot], arrived.at[slot])

    for step in range(min(DEPTH - 1, steps)):
        fetch(step, step).start()
    if cfg["last"]:
        max_ref[...] = jnp.full_like(max_ref, LOWEST)
        sum_ref[...] = jnp.zeros_like(sum_ref)
        hit_ref[...] = jnp.zeros_like(hit_ref)
    if cfg["labels"]:
        for block, (source, own) in zip(blocks, cfg["places"]):
            digits = jnp.transpose(block[:, cols:].astype(jnp.float32))
            whole = (digits[0:1] * BASE + digits[1:2]) * BASE + digits[2:3]
            here = pl.ds(own, block.shape[0])
            labels_out[:, here] = jnp.broadcast_to(whole, (SUB, block.shape[0])).astype(jnp.int32)
    places = cfg["places"]
    if cfg["join"]:
        rows = blocks[-2].shape[0]
        joined[:rows, :] = blocks[-2][:, :cols]
        joined[rows:, :] = blocks[-1][:, :cols]
        blocks, places = [*blocks[:-2], joined], places[:-1]

    def work(step, carry):
        slot = lax.rem(step, DEPTH)
        fetch(step, slot).wait()

        @pl.when(step + DEPTH - 1 < steps)
        def _():
            fetch(step + DEPTH - 1, lax.rem(step + DEPTH - 1, DEPTH)).start()

        span = pl.ds(pl.multiple_of(step * tile, tile), tile)
        for block, (source, own) in zip(blocks, places):
            rows = block.shape[0]
            part = lax.dot_general(
                ring[slot], block[:, :cols], (((1,), (1,)), ((), ())), preferred_element_type=jnp.float32
            )
            if cfg["adds"]:
                part = part + sums_in[span, pl.ds(source, rows)]
            if not cfg["last"]:
                out_ref[span, pl.ds(source, rows)] = part
                continue
            here = pl.ds(own, rows)
            groups = part.reshape(tile // SUB, SUB, rows)
            old = max_ref[:, here]
            new = jnp.maximum(old, jnp.max(groups, axis=0))
            near = labels_in[:1, pl.ds(source, rows)] - (cfg["offset_of"]() + step * tile)
            ids = lax.broadcasted_iota(jnp.int32, (tile, rows), 0)
            hits = jnp.where(ids == near, part, 0.0).reshape(tile // SUB, SUB, rows)
            sum_ref[:, here] = sum_ref[:, here] * jnp.exp(old - new) + jnp.sum(jnp.exp(groups - new[None]), axis=0)
            hit_ref[:, here] = hit_ref[:, here] + jnp.sum(hits, axis=0)
            max_ref[:, here] = new
        return carry

    lax.fori_loop(0, steps, work, 0)
    if cfg["last"]:
        kept = max_ref[...]
        top = jnp.max(kept, axis=0, keepdims=True)
        total = jnp.sum(sum_ref[...] * jnp.exp(kept - top), axis=0, keepdims=True)
        hit = jnp.sum(hit_ref[...], axis=0, keepdims=True)
        row = lax.broadcasted_iota(jnp.int32, kept.shape, 0)
        out_ref[...] = jnp.where(row == 0, top, jnp.where(row == 1, total, hit))


def head_pass(blocks, sources, table, col, cols, tokens, sums, adds, labels, emits, join):
    vocab = table.shape[0]
    last = labels is not None
    tile = max(t for t in range(16, MAX_TILE + 1, 16) if vocab % t == 0)
    rows = [b.shape[0] for b in blocks]
    owns = [sum(rows[:k]) for k in range(len(rows))]
    count = sum(rows)
    cfg = dict(
        places=list(zip(sources, owns)),
        has_sums=sums is not None,
        adds=adds,
        last=last,
        labels=emits,
        join=join,
        col=col,
        offset_of=lambda: (lax.axis_index("dp") * lax.axis_size("tensor") + lax.axis_index("tensor")) * vocab,
    )
    near = pl.BlockSpec(memory_space=pltpu.VMEM)
    args = [*blocks, table]
    in_specs = [near] * len(blocks) + [pl.BlockSpec(memory_space=pl.ANY)]
    aliases = {}
    if sums is not None:
        if not last:
            aliases[len(args)] = 0
        args.append(sums)
        in_specs.append(near)
    if last:
        args.append(labels)
        in_specs.append(near)
        out_shape = [jax.ShapeDtypeStruct((SUB, count), jnp.float32)]
    else:
        out_shape = [pltpu.VMEM((vocab, tokens), jnp.float32)]
        if emits:
            out_shape.append(jax.ShapeDtypeStruct((SUB, count), jnp.int32))
    scratch = [pltpu.VMEM((DEPTH, tile, cols), table.dtype), pltpu.SemaphoreType.DMA((DEPTH,))]
    if join:
        scratch.append(pltpu.VMEM((rows[-2] + rows[-1], cols), table.dtype))
    if last:
        scratch += [pltpu.VMEM((SUB, count), jnp.float32)] * 3
    return pl.pallas_call(
        functools.partial(head_kernel, cfg),
        out_shape=out_shape,
        in_specs=in_specs,
        out_specs=[near] * len(out_shape),
        scratch_shapes=scratch,
        input_output_aliases=aliases,
        compiler_params=pltpu.CompilerParams(vmem_limit_bytes=VMEM_LIMIT),
        cost_estimate=pl.CostEstimate(
            flops=2 * count * vocab * cols, bytes_accessed=2 * vocab * cols, transcendentals=0
        ),
    )(*args)


def swap(values, mask, devices):
    return lax.ppermute(values, AXES, [(i, i ^ mask) for i in range(devices)])


def meet(values, masks, devices):
    parts = [values]
    for take in range(1, 1 << len(masks)):
        mask = sum(m for j, m in enumerate(masks) if take >> j & 1)
        parts.append(swap(values, mask, devices))
    return parts


def merge(parts):
    top = functools.reduce(jnp.maximum, [p[0] for p in parts])
    totals = [p[1] * jnp.exp(p[0] - top) for p in parts]
    hits = [p[2] for p in parts]
    while len(totals) > 1:
        totals = [a + b for a, b in zip(totals[::2], totals[1::2])]
        hits = [a + b for a, b in zip(hits[::2], hits[1::2])]
    return jnp.stack([top, totals[0], hits[0]])


def body(mesh_shape, hidden, head_table, targets):
    devices = mesh_shape["dp"] * mesh_shape["tensor"]
    bits = devices.bit_length() - 1
    assert devices == 1 << bits and bits >= 2
    x_mask, y_mask = devices >> 1, 1
    z_masks = [1 << k for k in range(bits - 2, 0, -1)]
    own = hidden[0]
    own_count, width = own.shape
    tokens = own_count * devices
    quarter = tokens // 4
    half = quarter // 2

    ids = targets[0][:, None]
    digits = jnp.concatenate([ids // (BASE * BASE), ids // BASE % BASE, ids % BASE], axis=1).astype(own.dtype)
    digits = jnp.pad(digits, ((0, 0), (0, LANES - digits.shape[1])))

    units = width // LANES
    edges = [sum(WEIGHTS[:k]) * units // sum(WEIGHTS) * LANES for k in range(len(WEIGHTS) + 1)]
    sums, labels, stats = None, None, []
    for k, (begin, end) in enumerate(zip(edges, edges[1:])):
        last = k == len(WEIGHTS) - 1
        column = own[:, begin:end]
        if k == LABEL_CHUNK:
            column = jnp.concatenate([column, digits], axis=1)
        for start in range(0, len(z_masks), 2):
            column = jnp.concatenate(meet(column, z_masks[start : start + 2], devices), axis=0)
        from_x = swap(column, x_mask, devices)
        from_y = swap(column, y_mask, devices)
        far = [swap(from_x[:half], y_mask, devices), swap(from_y[half:], x_mask, devices)]
        groups = {
            "own": ([column], [0]),
            "rest": ([from_x, from_y, *far], [quarter, 2 * quarter, 3 * quarter, 3 * quarter + half]),
            "all": ([column, from_x, from_y, *far], [0, quarter, 2 * quarter, 3 * quarter, 3 * quarter + half]),
            "near": ([column, from_x, from_y], [0, quarter, 2 * quarter]),
            "far": (far, [3 * quarter, 3 * quarter + half]),
        }
        for group in GROUPS[k]:
            blocks, sources = groups[group]
            out = head_pass(
                blocks,
                sources,
                head_table,
                begin,
                end - begin,
                tokens,
                sums=sums,
                adds=k > 0,
                labels=labels if last else None,
                emits=k == LABEL_CHUNK,
                join=group in ("far", "rest", "all"),
            )
            if last:
                stats.append(out[0])
            else:
                sums = out[0]
            if k == LABEL_CHUNK:
                labels = out[1]

    state = jnp.concatenate([s[:3] for s in stats], axis=1)
    state = state.reshape((3, 2, 2) + (2,) * (bits - 2) + (own_count,))
    dims = [(x_mask, 2), (y_mask, 1)] + [(mask, len(z_masks) + 2 - j) for j, mask in enumerate(z_masks)]
    for pair in (dims[:2], *([d] for d in dims[2:])):
        parts = [state]
        for take in range(1, 1 << len(pair)):
            used = [pair[j] for j in range(len(pair)) if take >> j & 1]
            mask = sum(m for m, _ in used)
            got = swap(state, mask, devices)
            parts.append(jnp.flip(got, axis=tuple(d for _, d in used)))
        state = merge(parts)
    losses = state[0] + jnp.log(state[1]) - state[2]
    own_losses = losses[(0,) * bits]
    block_sums = jnp.sum(losses, axis=-1)
    for _ in range(bits):
        block_sums = block_sums[0] + block_sums[1]
    loss_sum = block_sums
    if mesh_shape["pipe"] == 2:
        loss_sum = loss_sum + lax.ppermute(loss_sum, "pipe", [(0, 1), (1, 0)])
    else:
        loss_sum = lax.psum(loss_sum, "pipe")
    mean_loss = loss_sum / (tokens * lax.axis_size("pipe"))
    return own_losses[None, :], mean_loss


def solution(mesh):
    in_specs = (P("pipe", AXES, None), P(AXES, None), P("pipe", AXES))
    out_specs = (P("pipe", AXES), P())

    def run(*args):
        return body(dict(mesh.shape), *args)

    return jax.shard_map(run, mesh=mesh, in_specs=in_specs, out_specs=out_specs, check_vma=False)
```
